32 devices in a mesh: groups: 2 (over y), seq: 2 (over core), mp: 8 (over z, x).
Axes of the slice: x: 2, y: 2, z: 4, core: 2. Of those that a mesh axis runs over, the one named last changes fastest.
Arguments:
- residual: bfloat16 [1024, 5376], P(('groups', 'seq', 'mp')), parts along dimension 0, may hold values from -6 to 6
- positions: int32 [1024], P(('groups', 'seq')), parts along dimension 0, may hold values from 0 to 383, as said below
- window_start: int32 [1024], P(('groups', 'seq')), parts along dimension 0, may hold values from 0 to 448, as said below
- input_gain: float32 [5376], replicated, may hold values from 0.1 to 1.9
- attention_gain: float32 [5376], replicated, may hold values from 0.1 to 1.9
- feedforward_gain: float32 [5376], replicated, may hold values from 0.1 to 1.9
- output_gain: float32 [5376], replicated, may hold values from 0.1 to 1.9
- query_weight: bfloat16 [5376, 4096], P(None, 'mp'), may hold values from -0.078125 to 0.078125
- key_weight: bfloat16 [5376, 2048], P(None, 'mp'), may hold values from -0.078125 to 0.078125
- value_weight: bfloat16 [5376, 2048], P(None, 'mp'), may hold values from -0.078125 to 0.078125
- output_weight: bfloat16 [4096, 5376], P('mp'), may hold values from -0.09375 to 0.09375
- gate_weight: bfloat16 [5376, 21504], P(None, 'mp'), may hold values from -0.078125 to 0.078125
- up_weight: bfloat16 [5376, 21504], P(None, 'mp'), may hold values from -0.078125 to 0.078125
- down_weight: bfloat16 [21504, 5376], P('mp'), may hold values from -0.0390625 to 0.0390625
Outputs:
- layer_out: bfloat16 [1024, 5376], P(('groups', 'seq', 'mp')), parts along dimension 0
The draws below stay inside these ranges and needn't reach their ends.
There are 2 independent parts, one for each index of `groups`. The reference program is written for one: setup_inputs(seed, part) draws one part's arguments, and reference() takes and returns one part's arrays. A program takes and returns all parts, laid end to end along the dimension named above; an argument that names none is the same for every part. Nothing has to cross between parts.
Inputs may be any that keep to these rules, and one draw needn't show every extreme that they name: positions[i] is i minus the first row of the document that holds row i; documents are consecutive runs of rows; one document of exactly 384 rows starts before row 32, the rows before it and the rows after it up to row 448 form shorter documents, and the last document starts at row 448. window_start[i] = max(first row of the document that holds row i, i - 191).
All inputs are finite; a program needn't handle non-finite values.
Results may differ from the reference program's by a relative error of at most 0.02.
Values may be sent and summed in bfloat16 or wider, within the bound.
A program may use at most 192 MiB of HBM per device.

```python
import jax
import jax.numpy as jnp
from jax import lax

D = 5376
FF = 21504
QH = 32
KVH = 16
HD = 128
WAL = 64
TOK_DEV = 256
WINDOW = 192
SEQ = 512


def document_starts(base_key):
    folded = jax.random.fold_in(base_key, 7)
    cut_key, flag_key = jax.random.split(folded)
    first_cut = jax.random.randint(cut_key, (), 1, TOK_DEV // 8)
    second_cut = first_cut + (SEQ - TOK_DEV // 2)
    third_cut = SEQ - TOK_DEV // 4
    row_index = jnp.arange(SEQ, dtype=jnp.int32)
    random_flags = jax.random.randint(flag_key, (SEQ,), 0, 2) == 1
    in_front = row_index < first_cut
    in_middle = (row_index > second_cut) & (row_index < third_cut)
    fixed_start = (row_index == 0) | (row_index == first_cut) | (row_index == second_cut) | (row_index == third_cut)
    is_start = fixed_start | (in_front | in_middle) & random_flags
    marked = jnp.where(is_start, row_index, 0).astype(jnp.int32)
    starts = lax.cummax(marked, axis=0)
    return (row_index, starts.astype(jnp.int32))


def draw_positions(key, part):
    row_index, starts = document_starts(key)
    return (row_index - starts).astype(jnp.int32)


def draw_window_start(key, part):
    row_index, starts = document_starts(key)
    return jnp.maximum(starts, row_index - WINDOW + 1).astype(jnp.int32)


def level_of(rng, shape, cuts, least, top_value):
    def one(axis_at, parts):
        draws = jax.random.uniform(jax.random.fold_in(jax.random.fold_in(rng, 6), axis_at), (parts,), jnp.float32, least / len(cuts), top_value / len(cuts))
        return jnp.repeat(jnp.exp(draws), shape[axis_at] // parts).reshape((-1,) + (1,) * (len(shape) - axis_at - 1))

    loudness = one(*cuts[0])
    for cut in cuts[1:]:
        loudness = loudness * one(*cut)
    return loudness


def centred(own_key, shape, width, limit, pieces=(), kind=jnp.bfloat16):
    values = width * jax.random.normal(own_key, shape, jnp.float32)
    if pieces:
        values = values * level_of(own_key, shape, pieces, -0.22, 0.18)
    return jnp.clip(values, -limit, limit).astype(kind)


def setup_inputs(seed: int = 0, part: int = 0) -> dict:
    keys = jax.random.split(jax.random.key(seed), 15)
    part_splits = jax.random.split(jax.random.fold_in(keys[14], part), 15)
    residual = centred(part_splits[0], (SEQ, D), 1.0, 6.0, ((0, 16),))
    positions = draw_positions(jax.random.fold_in(jax.random.fold_in(keys[14], part), 71), part)
    window_start = draw_window_start(jax.random.fold_in(jax.random.fold_in(keys[14], part), 71), part)
    input_gain = jnp.clip(1.0 + 0.18 * jax.random.normal(keys[3], (D,), jnp.float32), 0.1, 1.9)
    attention_gain = jnp.clip(1.0 + 0.18 * jax.random.normal(keys[4], (D,), jnp.float32), 0.1, 1.9)
    feedforward_gain = jnp.clip(1.0 + 0.18 * jax.random.normal(keys[5], (D,), jnp.float32), 0.1, 1.9)
    output_gain = jnp.clip(1.0 + 0.18 * jax.random.normal(keys[6], (D,), jnp.float32), 0.1, 1.9)
    query_weight = centred(keys[7], (D, QH * HD), D ** -0.5, 0.078125, ((1, 8),))
    key_weight = centred(keys[8], (D, KVH * HD), D ** -0.5, 0.078125, ((1, 8),))
    value_weight = centred(keys[9], (D, KVH * HD), D ** -0.5, 0.078125, ((1, 8),))
    output_weight = centred(keys[10], (QH * HD, D), (QH * HD) ** -0.5, 0.09375, ((0, 8),))
    gate_weight = centred(keys[11], (D, FF), D ** -0.5, 0.078125, ((1, 8),))
    up_weight = centred(keys[12], (D, FF), D ** -0.5, 0.078125, ((1, 8),))
    down_weight = centred(keys[13], (FF, D), FF ** -0.5, 0.0390625, ((0, 8),))
    return dict(residual=residual, positions=positions, window_start=window_start, input_gain=input_gain, attention_gain=attention_gain, feedforward_gain=feedforward_gain, output_gain=output_gain, query_weight=query_weight, key_weight=key_weight, value_weight=value_weight, output_weight=output_weight, gate_weight=gate_weight, up_weight=up_weight, down_weight=down_weight)


epsilon = 1e-06

def normalize(values_in, gain_row):
    widened = values_in.astype(jnp.float32)
    mean_square = lax.optimization_barrier(jnp.mean(widened * widened, axis=-1, keepdims=True))
    return widened * lax.rsqrt(mean_square + epsilon) * gain_row

def walsh_table(length):
    row_index = lax.broadcasted_iota(jnp.int32, (length, length), 0)
    column_index = lax.broadcasted_iota(jnp.int32, (length, length), 1)
    common = jnp.bitwise_and(row_index, column_index)
    parity = jnp.zeros((length, length), jnp.int32)
    for offset in range(max(length.bit_length() - 1, 0)):
        parity = parity + jnp.bitwise_and(jnp.right_shift(common, offset), 1)
    return (1 - 2 * jnp.bitwise_and(parity, 1)).astype(jnp.float32)

def angle_tables(positions, head_size):
    half_size = head_size // 2
    inverse = jnp.power(10000.0, -jnp.arange(half_size, dtype=jnp.float32) / half_size)
    angles = positions.astype(jnp.float32)[:, None] * inverse[None, :]
    return (jnp.cos(angles), jnp.sin(angles))

def rotary(linear, cosine_table, sine_table):
    row_count = linear.shape[0]
    half_size = cosine_table.shape[1]
    split_heads = linear.astype(jnp.float32).reshape(row_count, -1, 2 * half_size)
    front_half = split_heads[:, :, :half_size]
    back_half = split_heads[:, :, half_size:]
    cos_rows = cosine_table[:, None, :]
    sin_rows = sine_table[:, None, :]
    turned = jnp.concatenate([front_half * cos_rows - back_half * sin_rows, back_half * cos_rows + front_half * sin_rows], axis=-1)
    return turned.reshape(row_count, -1)

def reference(residual, positions, window_start, input_gain, attention_gain, feedforward_gain, output_gain, query_weight, key_weight, value_weight, output_weight, gate_weight, up_weight, down_weight):
    highest = lax.Precision.HIGHEST
    normed = normalize(residual, input_gain).astype(jnp.bfloat16)
    query_linear = jnp.dot(normed, query_weight, preferred_element_type=jnp.float32).astype(jnp.bfloat16)
    key_linear = jnp.dot(normed, key_weight, preferred_element_type=jnp.float32).astype(jnp.bfloat16)
    value_rows = jnp.dot(normed, value_weight, preferred_element_type=jnp.float32).astype(jnp.bfloat16)
    cosine_table, sine_table = angle_tables(positions, HD)
    queries = (rotary(query_linear, cosine_table, sine_table) * float(D // QH) ** (-0.5)).astype(jnp.bfloat16)
    key_rows = rotary(key_linear, cosine_table, sine_table).astype(jnp.bfloat16)
    row_index = jnp.arange(SEQ, dtype=jnp.int32)
    allowed = (row_index[None, :] <= row_index[:, None]) & (row_index[None, :] >= window_start[:, None])
    grouped_queries = queries.reshape(SEQ, KVH, 2, HD).transpose(1, 0, 2, 3)
    grouped_keys = key_rows.reshape(SEQ, KVH, HD).transpose(1, 0, 2)
    grouped_values = value_rows.reshape(SEQ, KVH, HD).transpose(1, 0, 2)

    def one_group(operands):
        group_queries, group_keys, group_values = operands
        scores = jnp.einsum('qtd,kd->tqk', group_queries.astype(jnp.float32), group_keys.astype(jnp.float32), precision=highest)
        scores = jnp.where(allowed[None], scores, -1e+30)
        largest = lax.optimization_barrier(jnp.max(scores, axis=-1, keepdims=True))
        exponent = jnp.exp(scores - largest)
        probabilities = (exponent / lax.optimization_barrier(jnp.sum(exponent, axis=-1, keepdims=True))).astype(jnp.bfloat16)
        combined = jnp.einsum('tqk,kd->qtd', probabilities.astype(jnp.float32), group_values.astype(jnp.float32), precision=highest)
        return combined.astype(jnp.bfloat16)
    attended = lax.map(one_group, (grouped_queries, grouped_keys, grouped_values))
    attended = attended.transpose(1, 0, 2, 3).reshape(SEQ, QH, HD)
    rotated = jnp.einsum('shd,de->she', attended.astype(jnp.float32), walsh_table(HD), precision=highest) * float(HD) ** (-0.5)
    rotated = rotated.astype(jnp.bfloat16).reshape(SEQ, QH * HD)
    attention_out = jnp.dot(rotated, output_weight, preferred_element_type=jnp.float32)
    first_sum = (residual.astype(jnp.float32) + normalize(attention_out, attention_gain)).astype(jnp.bfloat16)
    feed_input = normalize(first_sum, feedforward_gain).astype(jnp.bfloat16)
    gate_out = jnp.dot(feed_input, gate_weight, preferred_element_type=jnp.float32)
    up_out = jnp.dot(feed_input, up_weight, preferred_element_type=jnp.float32)
    activated = (jax.nn.gelu(gate_out, approximate=True) * up_out).astype(jnp.bfloat16)
    spread = jnp.einsum('sab,ac->scb', activated.reshape(SEQ, WAL, FF // WAL).astype(jnp.float32), walsh_table(WAL), precision=highest) * float(WAL) ** (-0.5)
    spread = spread.astype(jnp.bfloat16).reshape(SEQ, FF)
    down_out = jnp.dot(spread, down_weight, preferred_element_type=jnp.float32)
    return (first_sum.astype(jnp.float32) + normalize(down_out, output_gain)).astype(jnp.bfloat16)
```

```python
import functools

import jax
import jax.numpy as jnp
from jax import lax
from jax.experimental import pallas as pl
from jax.experimental.pallas import tpu as pltpu
from jax.sharding import PartitionSpec as P

D = 5376
FF = 21504
QH = 32
HD = 128
WAL = 64


epsilon = 1e-06


MESH = pl.DeviceIdType.MESH


def block_of(ref, index, rows):
    return ref.at[pl.ds(pl.multiple_of(index * rows, rows), rows)]


def send(source, target, send_sem, recv_sem, device):
    return pltpu.make_async_remote_copy(
        src_ref=source,
        dst_ref=target,
        send_sem=send_sem,
        recv_sem=recv_sem,
        device_id={"mp": device},
        device_id_type=MESH,
    )


def place(count):
    me = lax.axis_index("mp")
    column = lax.rem(me, 2)
    line = lax.div(me, 2)
    return me, column, line, count // 2, me + 1 - 2 * column


def greet(me, line, lines, peer):
    barrier = pltpu.get_barrier_semaphore()
    pl.semaphore_signal(barrier, inc=1, device_id={"mp": peer}, device_id_type=MESH)

    @pl.when(line > 0)
    def _():
        pl.semaphore_signal(barrier, inc=1, device_id={"mp": me - 2}, device_id_type=MESH)

    @pl.when(line < lines - 1)
    def _():
        pl.semaphore_signal(barrier, inc=1, device_id={"mp": me + 2}, device_id_type=MESH)

    beside = jnp.minimum(line, 1) + jnp.minimum(lines - 1 - line, 1)
    pl.semaphore_wait(barrier, 1 + beside)


def gather_kernel(count, own_ref, all_ref, xs, xr, us, ur, ds, dr):
    rows = own_ref.shape[0]
    me, column, line, lines, peer = place(count)
    greet(me, line, lines, peer)

    def across(origin, source):
        there = block_of(all_ref, origin * 2 + column, rows)
        return send(source, there, xs.at[origin], xr.at[origin], peer)

    def upward(origin, source):
        there = block_of(all_ref, origin * 2 + column, rows)
        return send(source, there, us.at[origin], ur.at[origin], me + 2)

    def downward(origin, source):
        there = block_of(all_ref, origin * 2 + column, rows)
        return send(source, there, ds.at[origin], dr.at[origin], me - 2)

    @pl.when(line < lines - 1)
    def _():
        upward(line, own_ref).start()

    @pl.when(line > 0)
    def _():
        downward(line, own_ref).start()

    across(line, own_ref).start()
    all_ref[pl.ds(pl.multiple_of(me * rows, rows), rows), :] = own_ref[...]
    for step in range(1, lines):

        @pl.when(line - step >= 0)
        def _():
            origin = line - step
            held = block_of(all_ref, origin * 2 + column, rows)
            upward(origin, held).wait_recv()

            @pl.when(line < lines - 1)
            def _():
                upward(origin, held).start()

            across(origin, held).start()

        @pl.when(line + step < lines)
        def _():
            origin = line + step
            held = block_of(all_ref, origin * 2 + column, rows)
            downward(origin, held).wait_recv()

            @pl.when(line > 0)
            def _():
                downward(origin, held).start()

            across(origin, held).start()

    for origin in range(lines):
        across(origin, own_ref).wait_send()
        there = block_of(all_ref, origin * 2 + 1 - column, rows)
        send(own_ref, there, xs.at[origin], xr.at[origin], peer).wait_recv()

        @pl.when((origin <= line) & (line < lines - 1))
        def _():
            upward(origin, own_ref).wait_send()

        @pl.when((origin >= line) & (line > 0))
        def _():
            downward(origin, own_ref).wait_send()


def gather_rows(own):
    count = lax.axis_size("mp")
    rows, width = own.shape
    if rows % 16 or count % 2 or count < 4:
        return lax.all_gather(own, "mp", axis=0, tiled=True)
    lines = count // 2
    return pl.pallas_call(
        functools.partial(gather_kernel, count),
        out_shape=jax.ShapeDtypeStruct((count * rows, width), own.dtype),
        in_specs=[pl.BlockSpec(memory_space=pltpu.VMEM)],
        out_specs=pl.BlockSpec(memory_space=pltpu.VMEM),
        scratch_shapes=[pltpu.SemaphoreType.DMA((lines,))] * 6,
        compiler_params=pltpu.CompilerParams(
            collective_id=0, has_side_effects=True, vmem_limit_bytes=16 * 1024 * 1024
        ),
    )(own)


def scatter_kernel(count, term_ref, sum_ref, xb, ub, db, sb, xs, xr, us, ur, ds, dr):
    rows, width = sum_ref.shape
    me, column, line, lines, peer = place(count)
    step_width = 768 if width % 768 == 0 else 128
    greet(me, line, lines, peer)

    def across(dest):
        mine = block_of(term_ref, dest * 2 + 1 - column, rows)
        return send(mine, xb.at[dest], xs.at[dest], xr.at[dest], peer)

    def upward(dest):
        return send(sb.at[dest], ub.at[dest], us.at[dest], ur.at[dest], me + 2)

    def downward(dest):
        return send(sb.at[dest], db.at[dest], ds.at[dest], dr.at[dest], me - 2)

    for away in range(lines - 1, -1, -1):

        @pl.when(line - away >= 0)
        def _():
            across(line - away).start()

        if away:

            @pl.when(line + away < lines)
            def _():
                across(line + away).start()

    def add(dest, arrived, target, index):
        first = pl.multiple_of((dest * 2 + column) * rows, rows)

        def some(i, carry):
            cols = pl.ds(pl.multiple_of(i * step_width, step_width), step_width)
            total = term_ref[pl.ds(first, rows), cols].astype(jnp.float32)
            total = total + xb[dest, :, cols].astype(jnp.float32)
            for ref in arrived:
                total = total + ref[dest, :, cols].astype(jnp.float32)
            if index:
                target[dest, :, cols] = total.astype(target.dtype)
            else:
                target[:, cols] = total
            return carry

        lax.fori_loop(0, width // step_width, some, 0)

    def go_up(dest):
        @pl.when(dest > line)
        def _():
            across(dest).wait_recv()

            @pl.when(line > 0)
            def _():
                upward(dest).wait_recv()
                add(dest, (ub,), sb, True)

            @pl.when(line == 0)
            def _():
                add(dest, (), sb, True)

            upward(dest).start()

    def go_down(dest):
        @pl.when(dest < line)
        def _():
            across(dest).wait_recv()

            @pl.when(line < lines - 1)
            def _():
                downward(dest).wait_recv()
                add(dest, (db,), sb, True)

            @pl.when(line == lines - 1)
            def _():
                add(dest, (), sb, True)

            downward(dest).start()

    for j in range(lines - 1):

        @pl.when(2 * line < lines)
        def _():
            go_up(lines - 1 - j)
            go_down(j)

        @pl.when(2 * line >= lines)
        def _():
            go_down(j)
            go_up(lines - 1 - j)

    across(line).wait_recv()

    @pl.when(line > 0)
    def _():
        upward(line).wait_recv()

    @pl.when(line < lines - 1)
    def _():
        downward(line).wait_recv()

    @pl.when((line > 0) & (line < lines - 1))
    def _():
        add(line, (ub, db), sum_ref, False)

    @pl.when(line == 0)
    def _():
        add(line, (db,), sum_ref, False)

    @pl.when(line == lines - 1)
    def _():
        add(line, (ub,), sum_ref, False)

    for dest in range(lines):
        across(dest).wait_send()

        @pl.when(dest > line)
        def _():
            upward(dest).wait_send()

        @pl.when(dest < line)
        def _():
            downward(dest).wait_send()


def scatter_rows(term):
    count = lax.axis_size("mp")
    rows, width = term.shape[0] // count, term.shape[1]
    if rows % 16 or count % 2 or count < 4:
        return lax.psum_scatter(term, "mp", scatter_dimension=0, tiled=True)
    lines = count // 2
    blocks = pltpu.VMEM((lines, rows, width), jnp.bfloat16)
    return pl.pallas_call(
        functools.partial(scatter_kernel, count),
        out_shape=jax.ShapeDtypeStruct((rows, width), jnp.float32),
        in_specs=[pl.BlockSpec(memory_space=pltpu.VMEM)],
        out_specs=pl.BlockSpec(memory_space=pltpu.VMEM),
        scratch_shapes=[blocks] * 4 + [pltpu.SemaphoreType.DMA((lines,))] * 6,
        compiler_params=pltpu.CompilerParams(
            collective_id=1, has_side_effects=True, vmem_limit_bytes=24 * 1024 * 1024
        ),
    )(term.astype(jnp.bfloat16))


def partner(block, axis, apart):
    count = lax.axis_size(axis)
    route = []
    for low in range(count):
        high = low | 1 << apart
        if high != low and high < count:
            route += [(low, high), (high, low)]
    return lax.ppermute(block, axis, route)


def for_sending(value):
    return jax.tree.map(lambda a: a.astype(jnp.bfloat16) if a.dtype == jnp.float32 else a, value)


def from_behind(block, axis, distance):
    devices = range(lax.axis_size(axis))
    route = [(i - distance, i) for i in devices if i - distance in devices]
    return lax.ppermute(block, axis, route)


def normalize(values_in, gain_row):
    widened = values_in.astype(jnp.float32)
    mean_square = jnp.mean(widened * widened, axis=-1, keepdims=True)
    return widened * lax.rsqrt(mean_square + epsilon) * gain_row


def walsh_table(length):
    row_index = lax.broadcasted_iota(jnp.int32, (length, length), 0)
    column_index = lax.broadcasted_iota(jnp.int32, (length, length), 1)
    common = jnp.bitwise_and(row_index, column_index)
    parity = jnp.zeros((length, length), jnp.int32)
    for offset in range(max(length.bit_length() - 1, 0)):
        parity = parity + jnp.bitwise_and(jnp.right_shift(common, offset), 1)
    return (1 - 2 * jnp.bitwise_and(parity, 1)).astype(jnp.float32)


def angle_tables(positions, head_size):
    half_size = head_size // 2
    inverse = jnp.power(10000.0, -jnp.arange(half_size, dtype=jnp.float32) / half_size)
    angles = positions.astype(jnp.float32)[:, None] * inverse[None, :]
    return (jnp.cos(angles), jnp.sin(angles))


def rotary(linear, cosine_table, sine_table):
    row_count = linear.shape[0]
    half_size = cosine_table.shape[1]
    split_heads = linear.astype(jnp.float32).reshape(row_count, -1, 2 * half_size)
    front_half = split_heads[:, :, :half_size]
    back_half = split_heads[:, :, half_size:]
    cos_rows = cosine_table[:, None, :]
    sin_rows = sine_table[:, None, :]
    turned = jnp.concatenate(
        [
            front_half * cos_rows - back_half * sin_rows,
            back_half * cos_rows + front_half * sin_rows,
        ],
        axis=-1,
    )
    return turned.reshape(row_count, -1)


def join_pair(own_part, theirs, upper_bit, axis_number):
    lower_part = jnp.where(upper_bit == 1, theirs, own_part)
    upper_part = jnp.where(upper_bit == 1, own_part, theirs)
    return jnp.concatenate([lower_part, upper_part], axis=axis_number)


def attend(queries, key_rows, value_rows, allowed):
    scores = jnp.einsum("qgtd,kgd->gtqk", queries, key_rows, preferred_element_type=jnp.float32)
    scores = jnp.where(allowed[None, None], scores, -1e30)
    largest = jnp.max(scores, axis=-1, keepdims=True)
    exponent = jnp.exp(scores - largest)
    probabilities = (exponent / jnp.sum(exponent, axis=-1, keepdims=True)).astype(jnp.bfloat16)
    combined = jnp.einsum(
        "gtqk,kgd->qgtd", probabilities, value_rows, preferred_element_type=jnp.float32
    )
    return combined.astype(jnp.bfloat16)


def body(
    residual,
    positions,
    window_start,
    input_gain,
    attention_gain,
    feedforward_gain,
    output_gain,
    query_weight,
    key_weight,
    value_weight,
    output_weight,
    gate_weight,
    up_weight,
    down_weight,
):
    model_count = lax.axis_size("mp")
    model_index = lax.axis_index("mp")
    block_index = lax.axis_index("seq")
    block_input = gather_rows(residual)
    block_length = block_input.shape[0]
    own_rows = block_length // model_count
    model_width = output_weight.shape[1]
    normed = normalize(block_input, input_gain).astype(jnp.bfloat16)
    cosine_table, sine_table = angle_tables(positions, HD)
    query_scale = float(D // QH) ** (-0.5)
    paired = model_count == 2 * QH
    if paired:
        half_rows = block_length // 2
        quarter_rows = block_length // 4
        low_bit = model_index % 2
        query_first = low_bit * half_rows
        query_cosine = lax.dynamic_slice_in_dim(cosine_table, query_first, half_rows, 0)
        query_sine = lax.dynamic_slice_in_dim(sine_table, query_first, half_rows, 0)
        partner_columns = partner(query_weight, "mp", 0)
        full_query = join_pair(query_weight, partner_columns, low_bit, 1)
        query_normed = lax.dynamic_slice_in_dim(normed, query_first, half_rows, 0)
        query_linear = jnp.dot(query_normed, full_query, preferred_element_type=jnp.float32).astype(
            jnp.bfloat16
        )
        key_full = key_weight
        value_full = value_weight
        for bit_number in range(2):
            upper_bit = jnp.right_shift(model_index, bit_number) % 2
            partner_key, partner_value = (
                partner(for_sending(key_full), "mp", bit_number).astype(key_full.dtype),
                partner(for_sending(value_full), "mp", bit_number).astype(value_full.dtype),
            )
            key_full = join_pair(key_full, partner_key, upper_bit, 1)
            value_full = join_pair(value_full, partner_value, upper_bit, 1)
        quarter_first = model_index % 4 * quarter_rows
        quarter_normed = lax.dynamic_slice_in_dim(normed, quarter_first, quarter_rows, 0)
        quarter_cosine = lax.dynamic_slice_in_dim(cosine_table, quarter_first, quarter_rows, 0)
        quarter_sine = lax.dynamic_slice_in_dim(sine_table, quarter_first, quarter_rows, 0)
        key_linear = jnp.dot(quarter_normed, key_full, preferred_element_type=jnp.float32).astype(
            jnp.bfloat16
        )
        key_part = rotary(key_linear, quarter_cosine, quarter_sine).astype(jnp.bfloat16)
        value_part = jnp.dot(quarter_normed, value_full, preferred_element_type=jnp.float32).astype(
            jnp.bfloat16
        )
        for bit_number in range(2):
            upper_bit = jnp.right_shift(model_index, bit_number) % 2
            partner_key, partner_value = (
                partner(for_sending(key_part), "mp", bit_number).astype(key_part.dtype),
                partner(for_sending(value_part), "mp", bit_number).astype(value_part.dtype),
            )
            key_part = join_pair(key_part, partner_key, upper_bit, 0)
            value_part = join_pair(value_part, partner_value, upper_bit, 0)
        key_rows = key_part
        value_rows = value_part
        group_count = 1
        query_count = half_rows
        queries = (rotary(query_linear, query_cosine, query_sine) * query_scale).astype(
            jnp.bfloat16
        )
        queries = queries.reshape(query_count, 1, 1, HD)
        own_window = lax.dynamic_slice_in_dim(window_start, query_first, half_rows, 0)
    else:
        query_first = 0
        query_count = block_length
        group_count = key_weight.shape[1] // HD
        query_linear = jnp.dot(normed, query_weight, preferred_element_type=jnp.float32).astype(
            jnp.bfloat16
        )
        key_linear = jnp.dot(normed, key_weight, preferred_element_type=jnp.float32).astype(
            jnp.bfloat16
        )
        key_rows = rotary(key_linear, cosine_table, sine_table).astype(jnp.bfloat16)
        value_rows = jnp.dot(normed, value_weight, preferred_element_type=jnp.float32).astype(
            jnp.bfloat16
        )
        queries = (rotary(query_linear, cosine_table, sine_table) * query_scale).astype(
            jnp.bfloat16
        )
        queries = queries.reshape(query_count, group_count, 2, HD)
        own_window = window_start
    previous_key, previous_value = from_behind((key_rows, value_rows), "seq", 1)
    all_keys = jnp.concatenate([previous_key, key_rows], axis=0).reshape(
        2 * block_length, group_count, HD
    )
    all_values = jnp.concatenate([previous_value, value_rows], axis=0).reshape(
        2 * block_length, group_count, HD
    )
    key_index = (block_index - 1) * block_length + jnp.arange(2 * block_length, dtype=jnp.int32)
    query_index = (
        block_index * block_length + query_first + jnp.arange(query_count, dtype=jnp.int32)
    )
    allowed = (key_index[None, :] <= query_index[:, None]) & (
        key_index[None, :] >= own_window[:, None]
    )
    attended = attend(queries, all_keys, all_values, allowed)
    head_walsh = walsh_table(HD).astype(jnp.bfloat16)
    rotated = jnp.einsum(
        "qgtd,de->qgte", attended, head_walsh, preferred_element_type=jnp.float32
    ) * float(HD) ** (-0.5)
    rotated = rotated.astype(jnp.bfloat16).reshape(query_count, -1)
    if paired:
        partner_rows = partner(output_weight, "mp", 0)
        full_output = join_pair(output_weight, partner_rows, low_bit, 0)
        half_term = jnp.dot(rotated, full_output, preferred_element_type=jnp.float32)
        padded = lax.dynamic_update_slice_in_dim(
            jnp.zeros((block_length, model_width), jnp.float32), half_term, query_first, 0
        )

        def attention_term(first_row, row_count):
            return lax.dynamic_slice_in_dim(padded, first_row, row_count, 0)

    else:

        def attention_term(first_row, row_count):
            picked = lax.dynamic_slice_in_dim(rotated, first_row, row_count, 0)
            return jnp.dot(picked, output_weight, preferred_element_type=jnp.float32)

    attention_rows = scatter_rows(attention_term(jnp.int32(0), lax.axis_size("mp") * own_rows))
    first_sum = (residual.astype(jnp.float32) + normalize(attention_rows, attention_gain)).astype(
        jnp.bfloat16
    )
    feed_own = normalize(first_sum, feedforward_gain).astype(jnp.bfloat16)
    feed_input = gather_rows(feed_own)
    gate_out = jnp.dot(feed_input, gate_weight, preferred_element_type=jnp.float32)
    up_out = jnp.dot(feed_input, up_weight, preferred_element_type=jnp.float32)
    activated = (jax.nn.gelu(gate_out, approximate=True) * up_out).astype(jnp.bfloat16)
    local_count = WAL // model_count
    block_width = FF // WAL
    grouped = activated.reshape(block_length, local_count, block_width)
    walsh_scale = float(WAL) ** (-0.5)
    full_table = walsh_table(WAL).astype(jnp.bfloat16)
    mixed_rows = (
        jnp.einsum(
            "rab,ac->rcb",
            lax.all_to_all(grouped, "mp", split_axis=0, concat_axis=1, tiled=True),
            full_table,
            preferred_element_type=jnp.float32,
        )
        * walsh_scale
    )
    spread = lax.all_to_all(
        mixed_rows.astype(jnp.bfloat16), "mp", split_axis=1, concat_axis=0, tiled=True
    )
    spread = spread.reshape(block_length, -1)
    picked = spread
    down_rows = scatter_rows(jnp.dot(picked, down_weight, preferred_element_type=jnp.float32))
    return (first_sum.astype(jnp.float32) + normalize(down_rows, output_gain)).astype(jnp.bfloat16)


def solution(mesh):
    placed = (
        P(("groups", "seq", "mp"), None),
        P(("groups", "seq")),
        P(("groups", "seq")),
        P(),
        P(),
        P(),
        P(),
        P(None, "mp"),
        P(None, "mp"),
        P(None, "mp"),
        P("mp", None),
        P(None, "mp"),
        P(None, "mp"),
        P("mp", None),
    )
    return jax.shard_map(
        body,
        mesh=mesh,
        in_specs=placed,
        out_specs=P(("groups", "seq", "mp"), None),
        check_vma=False,
    )
```

```python
import functools

import jax
import jax.numpy as jnp
from jax import lax
from jax.experimental import pallas as pl
from jax.experimental.pallas import tpu as pltpu
from jax.sharding import PartitionSpec as P

D = 5376
FF = 21504
QH = 32
HD = 128
WAL = 64


epsilon = 1e-06


MESH = pl.DeviceIdType.MESH


def block_of(ref, index, rows):
    return ref.at[pl.ds(pl.multiple_of(index * rows, rows), rows)]


def send(source, target, send_sem, recv_sem, device):
    return pltpu.make_async_remote_copy(
        src_ref=source,
        dst_ref=target,
        send_sem=send_sem,
        recv_sem=recv_sem,
        device_id={"mp": device},
        device_id_type=MESH,
    )


def place(count):
    me = lax.axis_index("mp")
    column = lax.rem(me, 2)
    line = lax.div(me, 2)
    return me, column, line, count // 2, me + 1 - 2 * column


def greet(me, line, lines, peer):
    barrier = pltpu.get_barrier_semaphore()
    pl.semaphore_signal(barrier, inc=1, device_id={"mp": peer}, device_id_type=MESH)

    @pl.when(line > 0)
    def _():
        pl.semaphore_signal(barrier, inc=1, device_id={"mp": me - 2}, device_id_type=MESH)

    @pl.when(line < lines - 1)
    def _():
        pl.semaphore_signal(barrier, inc=1, device_id={"mp": me + 2}, device_id_type=MESH)

    beside = jnp.minimum(line, 1) + jnp.minimum(lines - 1 - line, 1)
    pl.semaphore_wait(barrier, 1 + beside)


def gather_kernel(count, own_ref, all_ref, xs, xr, us, ur, ds, dr):
    rows = own_ref.shape[0]
    me, column, line, lines, peer = place(count)
    greet(me, line, lines, peer)

    def across(origin, source):
        there = block_of(all_ref, origin * 2 + column, rows)
        return send(source, there, xs.at[origin], xr.at[origin], peer)

    def upward(origin, source):
        there = block_of(all_ref, origin * 2 + column, rows)
        return send(source, there, us.at[origin], ur.at[origin], me + 2)

    def downward(origin, source):
        there = block_of(all_ref, origin * 2 + column, rows)
        return send(source, there, ds.at[origin], dr.at[origin], me - 2)

    @pl.when(line < lines - 1)
    def _():
        upward(line, own_ref).start()

    @pl.when(line > 0)
    def _():
        downward(line, own_ref).start()

    across(line, own_ref).start()
    all_ref[pl.ds(pl.multiple_of(me * rows, rows), rows), :] = own_ref[...]
    for step in range(1, lines):

        @pl.when(line - step >= 0)
        def _():
            origin = line - step
            held = block_of(all_ref, origin * 2 + column, rows)
            upward(origin, held).wait_recv()

            @pl.when(line < lines - 1)
            def _():
                upward(origin, held).start()

            across(origin, held).start()

        @pl.when(line + step < lines)
        def _():
            origin = line + step
            held = block_of(all_ref, origin * 2 + column, rows)
            downward(origin, held).wait_recv()

            @pl.when(line > 0)
            def _():
                downward(origin, held).start()

            across(origin, held).start()

    for origin in range(lines):
        across(origin, own_ref).wait_send()
        there = block_of(all_ref, origin * 2 + 1 - column, rows)
        send(own_ref, there, xs.at[origin], xr.at[origin], peer).wait_recv()

        @pl.when((origin <= line) & (line < lines - 1))
        def _():
            upward(origin, own_ref).wait_send()

        @pl.when((origin >= line) & (line > 0))
        def _():
            downward(origin, own_ref).wait_send()


def gather_rows(own):
    count = lax.axis_size("mp")
    rows, width = own.shape
    if rows % 16 or count % 2 or count < 4:
        return lax.all_gather(own, "mp", axis=0, tiled=True)
    lines = count // 2
    return pl.pallas_call(
        functools.partial(gather_kernel, count),
        out_shape=jax.ShapeDtypeStruct((count * rows, width), own.dtype),
        in_specs=[pl.BlockSpec(memory_space=pltpu.VMEM)],
        out_specs=pl.BlockSpec(memory_space=pltpu.VMEM),
        scratch_shapes=[pltpu.SemaphoreType.DMA((lines,))] * 6,
        compiler_params=pltpu.CompilerParams(
            collective_id=0, has_side_effects=True, vmem_limit_bytes=16 * 1024 * 1024
        ),
    )(own)


def scatter_kernel(count, term_ref, sum_ref, xb, ub, db, sb, xs, xr, us, ur, ds, dr):
    rows, width = sum_ref.shape
    me, column, line, lines, peer = place(count)
    step_width = 768 if width % 768 == 0 else 128
    greet(me, line, lines, peer)

    def across(dest):
        mine = block_of(term_ref, dest * 2 + 1 - column, rows)
        return send(mine, xb.at[dest], xs.at[dest], xr.at[dest], peer)

    def upward(dest):
        return send(sb.at[dest], ub.at[dest], us.at[dest], ur.at[dest], me + 2)

    def downward(dest):
        return send(sb.at[dest], db.at[dest], ds.at[dest], dr.at[dest], me - 2)

    for away in range(lines - 1, -1, -1):

        @pl.when(line - away >= 0)
        def _():
            across(line - away).start()

        if away:

            @pl.when(line + away < lines)
            def _():
                across(line + away).start()

    def add(dest, arrived, target, index):
        first = pl.multiple_of((dest * 2 + column) * rows, rows)

        def some(i, carry):
            cols = pl.ds(pl.multiple_of(i * step_width, step_width), step_width)
            total = term_ref[pl.ds(first, rows), cols].astype(jnp.float32)
            total = total + xb[dest, :, cols].astype(jnp.float32)
            for ref in arrived:
                total = total + ref[dest, :, cols].astype(jnp.float32)
            if index:
                target[dest, :, cols] = total.astype(target.dtype)
            else:
                target[:, cols] = total
            return carry

        lax.fori_loop(0, width // step_width, some, 0)

    def go_up(dest):
        @pl.when(dest > line)
        def _():
            across(dest).wait_recv()

            @pl.when(line > 0)
            def _():
                upward(dest).wait_recv()
                add(dest, (ub,), sb, True)

            @pl.when(line == 0)
            def _():
                add(dest, (), sb, True)

            upward(dest).start()

    def go_down(dest):
        @pl.when(dest < line)
        def _():
            across(dest).wait_recv()

            @pl.when(line < lines - 1)
            def _():
                downward(dest).wait_recv()
                add(dest, (db,), sb, True)

            @pl.when(line == lines - 1)
            def _():
                add(dest, (), sb, True)

            downward(dest).start()

    for j in range(lines - 1):

        @pl.when(2 * line < lines)
        def _():
            go_up(lines - 1 - j)
            go_down(j)

        @pl.when(2 * line >= lines)
        def _():
            go_down(j)
            go_up(lines - 1 - j)

    across(line).wait_recv()

    @pl.when(line > 0)
    def _():
        upward(line).wait_recv()

    @pl.when(line < lines - 1)
    def _():
        downward(line).wait_recv()

    @pl.when((line > 0) & (line < lines - 1))
    def _():
        add(line, (ub, db), sum_ref, False)

    @pl.when(line == 0)
    def _():
        add(line, (db,), sum_ref, False)

    @pl.when(line == lines - 1)
    def _():
        add(line, (ub,), sum_ref, False)

    for dest in range(lines):
        across(dest).wait_send()

        @pl.when(dest > line)
        def _():
            upward(dest).wait_send()

        @pl.when(dest < line)
        def _():
            downward(dest).wait_send()


def scatter_rows(term):
    count = lax.axis_size("mp")
    rows, width = term.shape[0] // count, term.shape[1]
    if rows % 16 or count % 2 or count < 4:
        return lax.psum_scatter(term, "mp", scatter_dimension=0, tiled=True)
    lines = count // 2
    blocks = pltpu.VMEM((lines, rows, width), jnp.bfloat16)
    return pl.pallas_call(
        functools.partial(scatter_kernel, count),
        out_shape=jax.ShapeDtypeStruct((rows, width), jnp.float32),
        in_specs=[pl.BlockSpec(memory_space=pltpu.VMEM)],
        out_specs=pl.BlockSpec(memory_space=pltpu.VMEM),
        scratch_shapes=[blocks] * 4 + [pltpu.SemaphoreType.DMA((lines,))] * 6,
        compiler_params=pltpu.CompilerParams(
            collective_id=1, has_side_effects=True, vmem_limit_bytes=24 * 1024 * 1024
        ),
    )(term.astype(jnp.bfloat16))


def hidden_kernel(count, tiles, feed_ref, gate_ref, up_ref, out_ref, act, got, ss, rs):
    rows = feed_ref.shape[0] // count
    width = gate_ref.shape[1]
    tile = pl.program_id(0)
    me = lax.axis_index("mp")

    @pl.when(tile == 0)
    def _():
        barrier = pltpu.get_barrier_semaphore()
        for k in range(1, count):
            other = lax.rem(me + k, count)
            pl.semaphore_signal(barrier, inc=1, device_id={"mp": other}, device_id_type=MESH)
        pl.semaphore_wait(barrier, count - 1)

    feed = feed_ref[...]
    gate_out = jnp.dot(feed, gate_ref[...], preferred_element_type=jnp.float32)
    up_out = jnp.dot(feed, up_ref[...], preferred_element_type=jnp.float32)
    act[tile] = (jax.nn.gelu(gate_out, approximate=True) * up_out).astype(jnp.bfloat16)

    def to(k, t):
        other = lax.rem(me + k, count)
        source = act.at[t, pl.ds(pl.multiple_of(other * rows, rows), rows), :]
        target = got.at[t, pl.ds(pl.multiple_of(me * rows, rows), rows), :]
        return send(source, target, ss.at[k, t], rs.at[k, t], other)

    for k in range(1, count):
        to(k, tile).start()
    own = pl.ds(pl.multiple_of(me * rows, rows), rows)
    got[tile, own, :] = act[tile, own, :]

    @pl.when(tile == tiles - 1)
    def _():
        for t in range(tiles):
            for k in range(1, count):
                to(k, t).wait_recv()
            out_ref[:, t * width : (t + 1) * width] = got[t]
        for t in range(tiles):
            for k in range(1, count):
                to(k, t).wait_send()


def hidden_rows(feed, gate_weight, up_weight):
    count = lax.axis_size("mp")
    length, depth = feed.shape
    hidden = gate_weight.shape[1]
    rows, tile = length // count, 384
    tiles = hidden // tile
    weights = pl.BlockSpec((depth, tile), lambda t: (0, t))
    return pl.pallas_call(
        functools.partial(hidden_kernel, count, tiles),
        grid=(tiles,),
        out_shape=jax.ShapeDtypeStruct((length, hidden), jnp.bfloat16),
        in_specs=[pl.BlockSpec((length, depth), lambda t: (0, 0)), weights, weights],
        out_specs=pl.BlockSpec((length, hidden), lambda t: (0, 0)),
        scratch_shapes=[
            pltpu.VMEM((tiles, length, tile), jnp.bfloat16),
            pltpu.VMEM((tiles, length, tile), jnp.bfloat16),
            pltpu.SemaphoreType.DMA((count, tiles)),
            pltpu.SemaphoreType.DMA((count, tiles)),
        ],
        compiler_params=pltpu.CompilerParams(
            collective_id=2,
            has_side_effects=True,
            dimension_semantics=("arbitrary",),
            vmem_limit_bytes=48 * 1024 * 1024,
        ),
    )(feed, gate_weight, up_weight)


def partner(block, axis, apart):
    count = lax.axis_size(axis)
    route = []
    for low in range(count):
        high = low | 1 << apart
        if high != low and high < count:
            route += [(low, high), (high, low)]
    return lax.ppermute(block, axis, route)


def for_sending(value):
    return jax.tree.map(lambda a: a.astype(jnp.bfloat16) if a.dtype == jnp.float32 else a, value)


def from_behind(block, axis, distance):
    devices = range(lax.axis_size(axis))
    route = [(i - distance, i) for i in devices if i - distance in devices]
    return lax.ppermute(block, axis, route)


def normalize(values_in, gain_row):
    widened = values_in.astype(jnp.float32)
    mean_square = jnp.mean(widened * widened, axis=-1, keepdims=True)
    return widened * lax.rsqrt(mean_square + epsilon) * gain_row


def walsh_table(length):
    row_index = lax.broadcasted_iota(jnp.int32, (length, length), 0)
    column_index = lax.broadcasted_iota(jnp.int32, (length, length), 1)
    common = jnp.bitwise_and(row_index, column_index)
    parity = jnp.zeros((length, length), jnp.int32)
    for offset in range(max(length.bit_length() - 1, 0)):
        parity = parity + jnp.bitwise_and(jnp.right_shift(common, offset), 1)
    return (1 - 2 * jnp.bitwise_and(parity, 1)).astype(jnp.float32)


def angle_tables(positions, head_size):
    half_size = head_size // 2
    inverse = jnp.power(10000.0, -jnp.arange(half_size, dtype=jnp.float32) / half_size)
    angles = positions.astype(jnp.float32)[:, None] * inverse[None, :]
    return (jnp.cos(angles), jnp.sin(angles))


def rotary(linear, cosine_table, sine_table):
    row_count = linear.shape[0]
    half_size = cosine_table.shape[1]
    split_heads = linear.astype(jnp.float32).reshape(row_count, -1, 2 * half_size)
    front_half = split_heads[:, :, :half_size]
    back_half = split_heads[:, :, half_size:]
    cos_rows = cosine_table[:, None, :]
    sin_rows = sine_table[:, None, :]
    turned = jnp.concatenate(
        [
            front_half * cos_rows - back_half * sin_rows,
            back_half * cos_rows + front_half * sin_rows,
        ],
        axis=-1,
    )
    return turned.reshape(row_count, -1)


def join_pair(own_part, theirs, upper_bit, axis_number):
    lower_part = jnp.where(upper_bit == 1, theirs, own_part)
    upper_part = jnp.where(upper_bit == 1, own_part, theirs)
    return jnp.concatenate([lower_part, upper_part], axis=axis_number)


def attend(queries, key_rows, value_rows, allowed):
    scores = jnp.einsum("qgtd,kgd->gtqk", queries, key_rows, preferred_element_type=jnp.float32)
    scores = jnp.where(allowed[None, None], scores, -1e30)
    largest = jnp.max(scores, axis=-1, keepdims=True)
    exponent = jnp.exp(scores - largest)
    probabilities = (exponent / jnp.sum(exponent, axis=-1, keepdims=True)).astype(jnp.bfloat16)
    combined = jnp.einsum(
        "gtqk,kgd->qgtd", probabilities, value_rows, preferred_element_type=jnp.float32
    )
    return combined.astype(jnp.bfloat16)


def body(
    residual,
    positions,
    window_start,
    input_gain,
    attention_gain,
    feedforward_gain,
    output_gain,
    query_weight,
    key_weight,
    value_weight,
    output_weight,
    gate_weight,
    up_weight,
    down_weight,
):
    model_count = lax.axis_size("mp")
    model_index = lax.axis_index("mp")
    block_index = lax.axis_index("seq")
    block_input = gather_rows(residual)
    block_length = block_input.shape[0]
    own_rows = block_length // model_count
    model_width = output_weight.shape[1]
    normed = normalize(block_input, input_gain).astype(jnp.bfloat16)
    cosine_table, sine_table = angle_tables(positions, HD)
    query_scale = float(D // QH) ** (-0.5)
    paired = model_count == 2 * QH
    if paired:
        half_rows = block_length // 2
        quarter_rows = block_length // 4
        low_bit = model_index % 2
        query_first = low_bit * half_rows
        query_cosine = lax.dynamic_slice_in_dim(cosine_table, query_first, half_rows, 0)
        query_sine = lax.dynamic_slice_in_dim(sine_table, query_first, half_rows, 0)
        partner_columns = partner(query_weight, "mp", 0)
        full_query = join_pair(query_weight, partner_columns, low_bit, 1)
        query_normed = lax.dynamic_slice_in_dim(normed, query_first, half_rows, 0)
        query_linear = jnp.dot(query_normed, full_query, preferred_element_type=jnp.float32).astype(
            jnp.bfloat16
        )
        key_full = key_weight
        value_full = value_weight
        for bit_number in range(2):
            upper_bit = jnp.right_shift(model_index, bit_number) % 2
            partner_key, partner_value = (
                partner(for_sending(key_full), "mp", bit_number).astype(key_full.dtype),
                partner(for_sending(value_full), "mp", bit_number).astype(value_full.dtype),
            )
            key_full = join_pair(key_full, partner_key, upper_bit, 1)
            value_full = join_pair(value_full, partner_value, upper_bit, 1)
        quarter_first = model_index % 4 * quarter_rows
        quarter_normed = lax.dynamic_slice_in_dim(normed, quarter_first, quarter_rows, 0)
        quarter_cosine = lax.dynamic_slice_in_dim(cosine_table, quarter_first, quarter_rows, 0)
        quarter_sine = lax.dynamic_slice_in_dim(sine_table, quarter_first, quarter_rows, 0)
        key_linear = jnp.dot(quarter_normed, key_full, preferred_element_type=jnp.float32).astype(
            jnp.bfloat16
        )
        key_part = rotary(key_linear, quarter_cosine, quarter_sine).astype(jnp.bfloat16)
        value_part = jnp.dot(quarter_normed, value_full, preferred_element_type=jnp.float32).astype(
            jnp.bfloat16
        )
        for bit_number in range(2):
            upper_bit = jnp.right_shift(model_index, bit_number) % 2
            partner_key, partner_value = (
                partner(for_sending(key_part), "mp", bit_number).astype(key_part.dtype),
                partner(for_sending(value_part), "mp", bit_number).astype(value_part.dtype),
            )
            key_part = join_pair(key_part, partner_key, upper_bit, 0)
            value_part = join_pair(value_part, partner_value, upper_bit, 0)
        key_rows = key_part
        value_rows = value_part
        group_count = 1
        query_count = half_rows
        queries = (rotary(query_linear, query_cosine, query_sine) * query_scale).astype(
            jnp.bfloat16
        )
        queries = queries.reshape(query_count, 1, 1, HD)
        own_window = lax.dynamic_slice_in_dim(window_start, query_first, half_rows, 0)
    else:
        query_first = 0
        query_count = block_length
        group_count = key_weight.shape[1] // HD
        query_linear = jnp.dot(normed, query_weight, preferred_element_type=jnp.float32).astype(
            jnp.bfloat16
        )
        key_linear = jnp.dot(normed, key_weight, preferred_element_type=jnp.float32).astype(
            jnp.bfloat16
        )
        key_rows = rotary(key_linear, cosine_table, sine_table).astype(jnp.bfloat16)
        value_rows = jnp.dot(normed, value_weight, preferred_element_type=jnp.float32).astype(
            jnp.bfloat16
        )
        queries = (rotary(query_linear, cosine_table, sine_table) * query_scale).astype(
            jnp.bfloat16
        )
        queries = queries.reshape(query_count, group_count, 2, HD)
        own_window = window_start
    previous_key, previous_value = from_behind((key_rows, value_rows), "seq", 1)
    all_keys = jnp.concatenate([previous_key, key_rows], axis=0).reshape(
        2 * block_length, group_count, HD
    )
    all_values = jnp.concatenate([previous_value, value_rows], axis=0).reshape(
        2 * block_length, group_count, HD
    )
    key_index = (block_index - 1) * block_length + jnp.arange(2 * block_length, dtype=jnp.int32)
    query_index = (
        block_index * block_length + query_first + jnp.arange(query_count, dtype=jnp.int32)
    )
    allowed = (key_index[None, :] <= query_index[:, None]) & (
        key_index[None, :] >= own_window[:, None]
    )
    attended = attend(queries, all_keys, all_values, allowed)
    head_walsh = walsh_table(HD).astype(jnp.bfloat16)
    rotated = jnp.einsum(
        "qgtd,de->qgte", attended, head_walsh, preferred_element_type=jnp.float32
    ) * float(HD) ** (-0.5)
    rotated = rotated.astype(jnp.bfloat16).reshape(query_count, -1)
    if paired:
        partner_rows = partner(output_weight, "mp", 0)
        full_output = join_pair(output_weight, partner_rows, low_bit, 0)
        half_term = jnp.dot(rotated, full_output, preferred_element_type=jnp.float32)
        padded = lax.dynamic_update_slice_in_dim(
            jnp.zeros((block_length, model_width), jnp.float32), half_term, query_first, 0
        )

        def attention_term(first_row, row_count):
            return lax.dynamic_slice_in_dim(padded, first_row, row_count, 0)

    else:

        def attention_term(first_row, row_count):
            picked = lax.dynamic_slice_in_dim(rotated, first_row, row_count, 0)
            return jnp.dot(picked, output_weight, preferred_element_type=jnp.float32)

    attention_rows = scatter_rows(attention_term(jnp.int32(0), lax.axis_size("mp") * own_rows))
    first_sum = (residual.astype(jnp.float32) + normalize(attention_rows, attention_gain)).astype(
        jnp.bfloat16
    )
    feed_own = normalize(first_sum, feedforward_gain).astype(jnp.bfloat16)
    feed_input = gather_rows(feed_own)
    local_count = WAL // model_count
    block_width = FF // WAL
    if own_rows % 16 == 0 and gate_weight.shape[1] % 384 == 0:
        gathered = hidden_rows(feed_input, gate_weight, up_weight)
        gathered = gathered.reshape(model_count, own_rows, local_count, block_width)
        exchanged = gathered.transpose(1, 0, 2, 3).reshape(own_rows, WAL, block_width)
    else:
        gate_out = jnp.dot(feed_input, gate_weight, preferred_element_type=jnp.float32)
        up_out = jnp.dot(feed_input, up_weight, preferred_element_type=jnp.float32)
        activated = (jax.nn.gelu(gate_out, approximate=True) * up_out).astype(jnp.bfloat16)
        grouped = activated.reshape(block_length, local_count, block_width)
        exchanged = lax.all_to_all(grouped, "mp", split_axis=0, concat_axis=1, tiled=True)
    walsh_scale = float(WAL) ** (-0.5)
    full_table = walsh_table(WAL).astype(jnp.bfloat16)
    mixed_rows = (
        jnp.einsum(
            "rab,ac->rcb",
            exchanged,
            full_table,
            preferred_element_type=jnp.float32,
        )
        * walsh_scale
    )
    spread = lax.all_to_all(
        mixed_rows.astype(jnp.bfloat16), "mp", split_axis=1, concat_axis=0, tiled=True
    )
    spread = spread.reshape(block_length, -1)
    picked = spread
    down_rows = scatter_rows(jnp.dot(picked, down_weight, preferred_element_type=jnp.float32))
    return (first_sum.astype(jnp.float32) + normalize(down_rows, output_gain)).astype(jnp.bfloat16)


def solution(mesh):
    placed = (
        P(("groups", "seq", "mp"), None),
        P(("groups", "seq")),
        P(("groups", "seq")),
        P(),
        P(),
        P(),
        P(),
        P(None, "mp"),
        P(None, "mp"),
        P(None, "mp"),
        P("mp", None),
        P(None, "mp"),
        P(None, "mp"),
        P("mp", None),
    )
    return jax.shard_map(
        body,
        mesh=mesh,
        in_specs=placed,
        out_specs=P(("groups", "seq", "mp"), None),
        check_vma=False,
    )
```
